32 devices in a mesh: groups: 2 (over y), tensor: 4 (over z), seq: 2 (over x), section: 2 (over core).
Axes of the slice: x: 2, y: 2, z: 4, core: 2. Of those that a mesh axis runs over, the one named last changes fastest.
Arguments:
- attn_out: bfloat16 [768, 8192], P(('groups', 'seq'), ('tensor', 'section')), parts along dimension 0, may hold values from -6 to 6
- residual: bfloat16 [768, 8192], P(('groups', 'seq'), ('tensor', 'section')), parts along dimension 0, may hold values from -120 to 120
- out_weight: bfloat16 [8192, 8192], P(('tensor', 'section')), may hold values from -0.09375 to 0.09375
- norm_gain: bfloat16 [8192], replicated, may hold values from 0.099609375 to 1.8984375
- gate_up: bfloat16 [8192, 2, 16384], P(None, None, ('tensor', 'seq', 'section')), may hold values from -0.0625 to 0.0625
Outputs:
- stream: bfloat16 [768, 8192], P(('groups', 'seq'), ('tensor', 'section')), parts along dimension 0
- hidden: bfloat16 [768, 16384], P('groups', ('tensor', 'seq', 'section')), parts along dimension 0
The draws below stay inside these ranges and needn't reach their ends.
There are 2 independent parts, one for each index of `groups`. The reference program is written for one: setup_inputs(seed, part) draws one part's arguments, and reference() takes and returns one part's arrays. A program takes and returns all parts, laid end to end along the dimension named above; an argument that names none is the same for every part. Nothing has to cross between parts.
All inputs are finite; a program needn't handle non-finite values.
Results may differ from the reference program's by a relative error of at most 0.012.
Values may be sent and summed in bfloat16 or wider, within the bound.
A program may use at most 192 MiB of HBM per device.

```python
import math
import jax
import jax.numpy as jnp
from jax import lax

D = 8192
FFW = 16384
ROWS = 384
N_TENSOR = 4
N_SECTION = 2


def draw_residual(key, part):
    first_key, second_key, third_key = jax.random.split(key, 3)
    column_ramp = jnp.exp(math.log(4.0) * jnp.arange(D, dtype=jnp.float32) / max(D - 1, 1))
    column_rough = jax.random.uniform(second_key, (D,), jnp.float32, 0.5, 1.5)
    row_scales = 0.3 * jnp.exp(jax.random.uniform(third_key, (ROWS, 1), jnp.float32, 0.0, math.log(10.0)))
    values_base = jnp.clip(jax.random.normal(first_key, (ROWS, D), jnp.float32), -6.0, 6.0)
    return (values_base * row_scales * column_ramp * column_rough).astype(jnp.bfloat16)


def with_spikes(array, rng, source, target, shards_of, factor):
    owner, partner = [(jnp.arange(array.shape[axis_at]) // (array.shape[axis_at] // shards_of)).reshape([-1 if axis == axis_at else 1 for axis in range(array.ndim)]) for axis_at in (source, target)]
    chosen = jax.random.permutation(rng, shards_of)[partner]
    strong = (owner == chosen) | (owner == (partner + shards_of // 2) % shards_of)
    return jnp.where(strong, factor * array, array)


def block_levels(own_key, dims, pieces, low, largest):
    gain, own = 1.0, jax.random.fold_in(own_key, 6)
    for dim, shards_of in pieces:
        draws = jnp.exp(jax.random.uniform(jax.random.fold_in(own, dim), (shards_of,), jnp.float32, low / len(pieces), largest / len(pieces)))
        gain = gain * jnp.repeat(draws, dims[dim] // shards_of).reshape([-1 if axis == dim else 1 for axis in range(len(dims))])
    return gain


def scatter_about(rng, dims, scale, reach, cuts=(), kind=jnp.bfloat16):
    drawn = jax.random.normal(rng, dims, jnp.float32) * scale
    if len(cuts) > 0:
        drawn = block_levels(rng, dims, cuts, -0.22, 0.18) * drawn
    return jnp.clip(drawn, min=-reach, max=reach).astype(kind)


def bell_draw_with(own_key, dims, width, reach, cuts, heavy, held_as=jnp.bfloat16):
    entries = width * jax.random.normal(own_key, dims, jnp.float32)
    if cuts:
        entries = entries * block_levels(own_key, dims, cuts, -0.22, 0.18)
    return jnp.clip(with_spikes(entries, jax.random.fold_in(own_key, 3), *heavy), -reach, reach).astype(held_as)


def setup_inputs(seed: int = 0, part: int = 0) -> dict:
    splits = jax.random.split(jax.random.key(seed), 6)
    part_splits = jax.random.split(jax.random.fold_in(splits[5], part), 6)
    attn_out = scatter_about(part_splits[0], (ROWS, D), 1.0, 6.0, ((0, 2), (1, 8)))
    residual = draw_residual(jax.random.fold_in(jax.random.fold_in(splits[5], part), 71), part)
    out_weight = bell_draw_with(splits[2], (D, D), D ** -0.5, 0.09375, ((0, 8),), (0, 1, 8, 2.0))
    norm_gain = jnp.clip(1.0 + 0.18 * jax.random.normal(splits[3], (D,), jnp.float32), 0.099609375, 1.8984375).astype(jnp.bfloat16)
    gate_up = scatter_about(splits[4], (D, 2, FFW), D ** -0.5, 0.0625, ((2, 16),))
    return dict(attn_out=attn_out, residual=residual, out_weight=out_weight, norm_gain=norm_gain, gate_up=gate_up)


epsilon = 1e-06

def tree_reduce(partials):
    current = partials
    while current.shape[0] > 1:
        current = (current[0::2].astype(jnp.float32) + current[1::2].astype(jnp.float32)).astype(jnp.bfloat16)
    return current[0]

def reference(attn_out, residual, out_weight, norm_gain, gate_up):
    shards = N_TENSOR * N_SECTION
    shard_width = D // shards
    col_block = math.gcd(D, 512)
    inputs_3d = attn_out.astype(jnp.float32).reshape(ROWS, shards, shard_width)
    columns = out_weight.reshape(D, D // col_block, col_block).transpose(1, 0, 2)

    def one_block(weight_cols):
        split_weight = weight_cols.astype(jnp.float32).reshape(shards, shard_width, col_block)
        partials = jnp.einsum('rpd,pdc->prc', inputs_3d, split_weight, precision=lax.Precision.HIGHEST).astype(jnp.bfloat16)
        return tree_reduce(partials)
    projected = lax.map(one_block, columns).transpose(1, 0, 2).reshape(ROWS, D)
    stream = (projected.astype(jnp.float32) + residual.astype(jnp.float32)).astype(jnp.bfloat16)
    stream_wide = stream.astype(jnp.float32)
    mean_square = lax.optimization_barrier(jnp.sum(stream_wide * stream_wide, axis=1, keepdims=True)) / D
    normed = (stream_wide * lax.rsqrt(mean_square + epsilon) * norm_gain.astype(jnp.float32)).astype(jnp.bfloat16)
    products = jnp.dot(normed, gate_up.reshape(D, 2 * FFW), preferred_element_type=jnp.float32).reshape(ROWS, 2, FFW)
    hidden = (jax.nn.silu(products[:, 0]) * products[:, 1]).astype(jnp.bfloat16)
    return (stream, hidden)
```

```python
import jax
import jax.numpy as jnp
from jax import lax
from jax.experimental import pallas as pl
from jax.experimental.pallas import tpu as pltpu
from jax.sharding import PartitionSpec as P

D = 8192


epsilon = 1e-06


def partner(x, axis, distance):
    return lax.ppermute(x, axis, [(i, i ^ 1 << distance) for i in range(lax.axis_size(axis))])


def local(attn_out, residual, out_weight, norm_gain, gate_up):
    axis_size = lax.axis_size(("tensor", "section"))
    position = lax.axis_index(("tensor", "section"))
    row_count, shard_width = attn_out.shape
    partial_value = jnp.dot(attn_out, out_weight, preferred_element_type=jnp.float32).astype(
        jnp.bfloat16
    )
    blocked = partial_value.reshape(row_count, axis_size, shard_width)
    for level_index in range(axis_size.bit_length() - 1):
        paired = blocked.reshape(row_count, blocked.shape[1] // 2, 2, shard_width)
        my_bit = position >> level_index & 1
        kept_half = lax.dynamic_index_in_dim(paired, my_bit, 2, keepdims=False)
        sent_half = lax.dynamic_index_in_dim(paired, 1 - my_bit, 2, keepdims=False)
        received = partner(sent_half, ("tensor", "section"), level_index)
        blocked = (kept_half.astype(jnp.float32) + received.astype(jnp.float32)).astype(
            jnp.bfloat16
        )
    projected = blocked.reshape(row_count, shard_width)
    stream = (projected.astype(jnp.float32) + residual.astype(jnp.float32)).astype(jnp.bfloat16)
    full_stream = lax.all_gather(stream, ("tensor", "section"), axis=1, tiled=True).astype(
        jnp.float32
    )
    totals = jnp.sum(full_stream * full_stream, axis=1, keepdims=True)
    normed_rows = (
        full_stream * lax.rsqrt(totals / D + epsilon) * norm_gain.astype(jnp.float32)
    ).astype(jnp.bfloat16)
    hidden_cols = gate_up.shape[2]
    local_weight = gate_up.reshape(D, 2 * hidden_cols)
    row_block = lax.all_gather(normed_rows, "seq", axis=0, tiled=True)
    products = jnp.dot(row_block, local_weight, preferred_element_type=jnp.float32)
    products = products.reshape(row_block.shape[0], 2, hidden_cols)
    hidden = (jax.nn.silu(products[:, 0]) * products[:, 1]).astype(jnp.bfloat16)
    return (stream, hidden)


CHUNKS = 4
RAW_SLOTS = 4
ORDER = (1, 3, 0, 2)


def fused_kernel(
    attn_ref,
    residual_ref,
    gain_ref,
    weight_hbm,
    gate_up_hbm,
    stream_ref,
    hidden_ref,
    weight_ring,
    raw_ring,
    weights,
    sent_part,
    kept_part,
    got0,
    got1,
    got2,
    blocks,
    scaled,
    acc,
    squares,
    weight_sem,
    raw_sem,
    send0,
    recv0,
    send1,
    recv1,
    send2,
    recv2,
    send_right,
    send_left,
    send_seq,
    send_own,
    send_other,
    recv_block,
):
    t = lax.axis_index("tensor")
    q = lax.axis_index("seq")
    s = lax.axis_index("section")
    nt = lax.axis_size("tensor")
    rows, width = attn_ref.shape
    sub = width // CHUNKS
    n_block = 2 * nt
    hidden_cols = hidden_ref.shape[1]
    depth = weights.shape[1]
    f32, bf16 = jnp.float32, jnp.bfloat16

    def relative(r):
        return ((t // 2 + r // 2) % 2) * 2 + (t + r % 2) % 2

    def remote(src, dst, ssem, rsem, **where):
        return pltpu.make_async_remote_copy(
            src_ref=src,
            dst_ref=dst,
            send_sem=ssem,
            recv_sem=rsem,
            device_id=where,
            device_id_type=pl.DeviceIdType.MESH,
        )

    def weight_copy(c, j, half):
        section = (1 - s) if half == 0 else s
        column = (relative(ORDER[j]) * 2 + section) * width + c * sub
        return pltpu.make_async_copy(
            weight_hbm.at[:, pl.ds(pl.multiple_of(column, sub), sub)],
            weight_ring.at[2 * j + half],
            weight_sem.at[2 * j + half],
        )

    def raw_copy(k):
        start = (k % n_block) * width + (k // n_block) * sub
        slot = k % RAW_SLOTS
        return pltpu.make_async_copy(
            gate_up_hbm.at[pl.ds(pl.multiple_of(start, sub), sub)],
            raw_ring.at[slot],
            raw_sem.at[slot],
        )

    def copy0(c, r):
        return remote(
            sent_part.at[c, r], got0.at[c, r], send0.at[c, r], recv0.at[c, r], section=1 - s
        )

    def copy1(c, h):
        return remote(
            kept_part.at[c, 2 * h + 1],
            got1.at[c, h],
            send1.at[c, h],
            recv1.at[c, h],
            tensor=relative(1),
        )

    def copy2(c):
        return remote(
            kept_part.at[c, 2], got2.at[c], send2.at[c], recv2.at[c], tensor=relative(2)
        )

    def copy_block(qq, c, o, sems, **where):
        b = o * 2 + s
        here = blocks.at[qq, c, b]
        return remote(here, here, sems.at[c, o], recv_block.at[qq, c, b], **where)

    def await_block(qq, c, b):
        here = blocks.at[qq, c, b]
        remote(
            here, here, send_own.at[c, 0], recv_block.at[qq, c, b], section=1 - s
        ).wait_recv()

    for j in range(4):
        for half in range(2):
            weight_copy(0, j, half).start()
    barrier = pltpu.get_barrier_semaphore()
    for d in range(1, nt):
        pl.semaphore_signal(barrier, inc=1, device_id={"tensor": (t + d) % nt}, device_id_type=pl.DeviceIdType.MESH)
    pl.semaphore_signal(barrier, inc=1, device_id={"seq": 1 - q}, device_id_type=pl.DeviceIdType.MESH)
    pl.semaphore_signal(barrier, inc=1, device_id={"section": 1 - s}, device_id_type=pl.DeviceIdType.MESH)
    for k in range(RAW_SLOTS):
        raw_copy(k).start()
    pl.semaphore_wait(barrier, nt + 1)

    def project(c):
        for j, r in enumerate(ORDER):
            for half in range(2):
                weight_copy(c, j, half).wait()
                part = jnp.dot(
                    attn_ref[...], weight_ring[2 * j + half], preferred_element_type=f32
                ).astype(bf16)
                (sent_part, kept_part)[half][c, r] = part

                @pl.when(c + 1 < CHUNKS)
                def _():
                    weight_copy(c + 1, j, half).start()

                if half == 0:
                    copy0(c, r).start()

    def add_section(c):
        for r in ORDER:
            copy0(c, r).wait_recv()
            kept_part[c, r] = (
                kept_part[c, r].astype(f32) + got0[c, r].astype(f32)
            ).astype(bf16)
            if r % 2:
                copy1(c, r // 2).start()

    def unpack(c):
        @pl.loop(0, n_block)
        def _(b):
            k = c * n_block + b
            raw_copy(k).wait()
            both = pltpu.einshape("kgn->gkn", raw_ring[k % RAW_SLOTS])
            place = pl.ds(pl.multiple_of(b * sub, sub), sub)
            weights[c, place, :hidden_cols] = both[0]
            weights[c, place, hidden_cols:] = both[1]

            @pl.when(k + RAW_SLOTS < CHUNKS * n_block)
            def _():
                raw_copy(k + RAW_SLOTS).start()

    def add_near(c):
        for h in (1, 0):
            copy1(c, h).wait_recv()
            kept_part[c, 2 * h] = (
                kept_part[c, 2 * h].astype(f32) + got1[c, h].astype(f32)
            ).astype(bf16)
            if h:
                copy2(c).start()

    def finish_stream(c):
        copy2(c).wait_recv()
        projected = (kept_part[c, 0].astype(f32) + got2[c].astype(f32)).astype(bf16)
        columns = pl.ds(pl.multiple_of(c * sub, sub), sub)
        stream = (projected.astype(f32) + residual_ref[:, columns].astype(f32)).astype(bf16)
        blocks[q, c, t * 2 + s] = stream
        stream_ref[:, columns] = stream

        @pl.when(t < nt - 1)
        def _():
            copy_block(q, c, t, send_right, tensor=t + 1).start()

        @pl.when(t > 0)
        def _():
            copy_block(q, c, t, send_left, tensor=t - 1).start()

        copy_block(q, c, t, send_seq, seq=1 - q).start()
        copy_block(q, c, t, send_own, section=1 - s).start()

    def forward(c, d):
        @pl.when(t >= d)
        def _():
            o = t - d
            await_block(q, c, o * 2 + s)

            @pl.when(t < nt - 1)
            def _():
                copy_block(q, c, o, send_right, tensor=t + 1).start()

            copy_block(q, c, o, send_seq, seq=1 - q).start()
            copy_block(q, c, o, send_own, section=1 - s).start()

        @pl.when(t + d < nt)
        def _():
            o = t + d
            await_block(q, c, o * 2 + s)

            @pl.when(t > 0)
            def _():
                copy_block(q, c, o, send_left, tensor=t - 1).start()

            copy_block(q, c, o, send_seq, seq=1 - q).start()
            copy_block(q, c, o, send_own, section=1 - s).start()

    def hand_over(c, d):
        def one(o):
            await_block(1 - q, c, o * 2 + s)
            copy_block(1 - q, c, o, send_other, section=1 - s).start()

        if d == 0:
            one(t)
        else:

            @pl.when(t >= d)
            def _():
                one(t - d)

            @pl.when(t + d < nt)
            def _():
                one(t + d)

    def multiply(qq, c):
        for o in range(nt):
            await_block(qq, c, o * 2 + 1 - s)

        @pl.loop(0, n_block)
        def _(b):
            x = blocks[qq, c, b].astype(f32)
            gain = gain_ref[:, pl.ds(pl.multiple_of(b * width + c * sub, sub), sub)].astype(f32)
            scaled[:, pl.ds(pl.multiple_of(b * sub, sub), sub)] = (x * gain).astype(bf16)
            square = x * x
            total = square[:, :128]
            for k in range(1, sub // 128):
                total = total + square[:, k * 128 : (k + 1) * 128]
            squares[qq] += total

        tile = 512

        @pl.loop(0, 2 * hidden_cols // tile)
        def _(n):
            columns = pl.ds(pl.multiple_of(n * tile, tile), tile)
            acc[qq, :, columns] += jnp.dot(
                scaled[...], weights[c, :, columns], preferred_element_type=f32
            )

    acc[...] = jnp.zeros_like(acc)
    squares[...] = jnp.zeros_like(squares)
    stages = (
        (0, project),
        (0, add_section),
        (1, add_near),
        (2, finish_stream),
        (3, lambda c: forward(c, 1)),
        (4, lambda c: forward(c, 2)),
        (5, lambda c: forward(c, 3)),
        (3, lambda c: hand_over(c, 0)),
        (4, lambda c: hand_over(c, 1)),
        (5, lambda c: hand_over(c, 2)),
        (6, lambda c: hand_over(c, 3)),
        (0, unpack),
        (6, lambda c: multiply(q, c)),
        (7, lambda c: multiply(1 - q, c)),
    )

    @pl.loop(0, CHUNKS + 7)
    def _(step):
        for lag, stage in stages:

            @pl.when(jnp.logical_and(step >= lag, step < lag + CHUNKS))
            def _():
                stage(step - lag)

    for qq in range(2):
        mean_square = jnp.sum(squares[qq], axis=1, keepdims=True) / (n_block * width)
        scale = lax.rsqrt(mean_square + epsilon)
        tile = 256

        @pl.loop(0, hidden_cols // tile)
        def _(n):
            gate = acc[qq, :, pl.ds(pl.multiple_of(n * tile, tile), tile)] * scale
            up = acc[qq, :, pl.ds(pl.multiple_of(hidden_cols + n * tile, tile), tile)] * scale
            hidden_ref[qq * rows : (qq + 1) * rows, pl.ds(pl.multiple_of(n * tile, tile), tile)] = (
                gate / (1.0 + jnp.exp(-gate)) * up
            ).astype(bf16)

    @pl.loop(0, CHUNKS)
    def _(c):
        for r in range(4):
            copy0(c, r).wait_send()
        for h in range(2):
            copy1(c, h).wait_send()
        copy2(c).wait_send()
        for o in range(nt):
            copy_block(q, c, o, send_seq, seq=1 - q).wait_send()
            copy_block(q, c, o, send_own, section=1 - s).wait_send()
            copy_block(1 - q, c, o, send_other, section=1 - s).wait_send()

            @pl.when(jnp.logical_and(o <= t, t < nt - 1))
            def _():
                copy_block(q, c, o, send_right, tensor=(t + 1) % nt).wait_send()

            @pl.when(jnp.logical_and(o >= t, t > 0))
            def _():
                copy_block(q, c, o, send_left, tensor=(t + nt - 1) % nt).wait_send()


def fused(attn_out, residual, out_weight, norm_gain, gate_up):
    rows, width = attn_out.shape
    nt = lax.axis_size("tensor")
    hidden_cols = gate_up.shape[2]
    sub = width // CHUNKS
    depth = gate_up.shape[0] // CHUNKS
    vmem = pl.BlockSpec(memory_space=pltpu.VMEM)
    hbm = pl.BlockSpec(memory_space=pl.ANY)
    dma = pltpu.SemaphoreType.DMA
    bf16, f32 = jnp.bfloat16, jnp.float32
    return pl.pallas_call(
        fused_kernel,
        name="layer_window",
        out_shape=(
            jax.ShapeDtypeStruct((rows, width), bf16),
            jax.ShapeDtypeStruct((2 * rows, hidden_cols), bf16),
        ),
        in_specs=[vmem, vmem, vmem, hbm, hbm],
        out_specs=(vmem, vmem),
        scratch_shapes=[
            pltpu.VMEM((8, width, sub), bf16),
            pltpu.VMEM((RAW_SLOTS, sub, 2, hidden_cols), bf16),
            pltpu.VMEM((CHUNKS, depth, 2 * hidden_cols), bf16),
            pltpu.VMEM((CHUNKS, 4, rows, sub), bf16),
            pltpu.VMEM((CHUNKS, 4, rows, sub), bf16),
            pltpu.VMEM((CHUNKS, 4, rows, sub), bf16),
            pltpu.VMEM((CHUNKS, 2, rows, sub), bf16),
            pltpu.VMEM((CHUNKS, rows, sub), bf16),
            pltpu.VMEM((2, CHUNKS, 2 * nt, rows, sub), bf16),
            pltpu.VMEM((rows, depth), bf16),
            pltpu.VMEM((2, rows, 2 * hidden_cols), f32),
            pltpu.VMEM((2, rows, 128), f32),
            dma((8,)),
            dma((RAW_SLOTS,)),
            dma((CHUNKS, 4)),
            dma((CHUNKS, 4)),
            dma((CHUNKS, 2)),
            dma((CHUNKS, 2)),
            dma((CHUNKS,)),
            dma((CHUNKS,)),
            dma((CHUNKS, nt)),
            dma((CHUNKS, nt)),
            dma((CHUNKS, nt)),
            dma((CHUNKS, nt)),
            dma((CHUNKS, nt)),
            dma((2, CHUNKS, 2 * nt)),
        ],
        compiler_params=pltpu.CompilerParams(
            collective_id=0, has_side_effects=True, vmem_limit_bytes=66 * 1024 * 1024 - 2 * 1024 * 1024 - 65536
        ),
    )(attn_out, residual, norm_gain.reshape(1, -1), out_weight, gate_up)


def fits_fused(mesh, attn_out, gate_up):
    rows, width = attn_out.shape
    return (
        (mesh.shape["tensor"], mesh.shape["seq"], mesh.shape["section"]) == (4, 2, 2)
        and rows % 16 == 0
        and width % (128 * CHUNKS) == 0
        and gate_up.shape[2] % 256 == 0
        and 2 * gate_up.size <= 34 * 1024 * 1024
        and rows * width <= 192 * 1024
    )


def solution(mesh):
    placed = (
        P(("groups", "seq"), ("tensor", "section")),
        P(("groups", "seq"), ("tensor", "section")),
        P(("tensor", "section"), None),
        P(),
        P(None, None, ("tensor", "seq", "section")),
    )
    def step(*args):
        return (fused if fits_fused(mesh, args[0], args[4]) else local)(*args)

    return jax.shard_map(
        step,
        mesh=mesh,
        in_specs=placed,
        out_specs=(
            P(("groups", "seq"), ("tensor", "section")),
            P("groups", ("tensor", "seq", "section")),
        ),
        check_vma=False,
    )
```

```python
import jax
import jax.numpy as jnp
from jax import lax
from jax.experimental import pallas as pl
from jax.experimental.pallas import tpu as pltpu
from jax.sharding import PartitionSpec as P

D = 8192


epsilon = 1e-06


def partner(x, axis, distance):
    return lax.ppermute(x, axis, [(i, i ^ 1 << distance) for i in range(lax.axis_size(axis))])


def local(attn_out, residual, out_weight, norm_gain, gate_up):
    axis_size = lax.axis_size(("tensor", "section"))
    position = lax.axis_index(("tensor", "section"))
    row_count, shard_width = attn_out.shape
    partial_value = jnp.dot(attn_out, out_weight, preferred_element_type=jnp.float32).astype(
        jnp.bfloat16
    )
    blocked = partial_value.reshape(row_count, axis_size, shard_width)
    for level_index in range(axis_size.bit_length() - 1):
        paired = blocked.reshape(row_count, blocked.shape[1] // 2, 2, shard_width)
        my_bit = position >> level_index & 1
        kept_half = lax.dynamic_index_in_dim(paired, my_bit, 2, keepdims=False)
        sent_half = lax.dynamic_index_in_dim(paired, 1 - my_bit, 2, keepdims=False)
        received = partner(sent_half, ("tensor", "section"), level_index)
        blocked = (kept_half.astype(jnp.float32) + received.astype(jnp.float32)).astype(
            jnp.bfloat16
        )
    projected = blocked.reshape(row_count, shard_width)
    stream = (projected.astype(jnp.float32) + residual.astype(jnp.float32)).astype(jnp.bfloat16)
    full_stream = lax.all_gather(stream, ("tensor", "section"), axis=1, tiled=True).astype(
        jnp.float32
    )
    totals = jnp.sum(full_stream * full_stream, axis=1, keepdims=True)
    normed_rows = (
        full_stream * lax.rsqrt(totals / D + epsilon) * norm_gain.astype(jnp.float32)
    ).astype(jnp.bfloat16)
    hidden_cols = gate_up.shape[2]
    local_weight = gate_up.reshape(D, 2 * hidden_cols)
    row_block = lax.all_gather(normed_rows, "seq", axis=0, tiled=True)
    products = jnp.dot(row_block, local_weight, preferred_element_type=jnp.float32)
    products = products.reshape(row_block.shape[0], 2, hidden_cols)
    hidden = (jax.nn.silu(products[:, 0]) * products[:, 1]).astype(jnp.bfloat16)
    return (stream, hidden)


CHUNKS = 4
RAW_SLOTS = 4
ORDER = (1, 3, 0, 2)


def fused_kernel(
    attn_ref,
    residual_ref,
    gain_ref,
    weight_hbm,
    gate_up_hbm,
    stream_ref,
    hidden_ref,
    weight_ring,
    raw_ring,
    weights,
    sent_part,
    kept_part,
    got0,
    got1,
    got2,
    blocks,
    scaled,
    acc,
    squares,
    weight_sem,
    raw_sem,
    send0,
    recv0,
    send1,
    recv1,
    send2,
    recv2,
    send_right,
    send_left,
    send_seq,
    send_own,
    send_other,
    recv_block,
):
    t = lax.axis_index("tensor")
    q = lax.axis_index("seq")
    s = lax.axis_index("section")
    nt = lax.axis_size("tensor")
    rows, width = attn_ref.shape
    sub = width // CHUNKS
    n_block = 2 * nt
    hidden_cols = hidden_ref.shape[1]
    depth = weights.shape[1]
    f32, bf16 = jnp.float32, jnp.bfloat16

    def relative(r):
        return ((t // 2 + r // 2) % 2) * 2 + (t + r % 2) % 2

    def remote(src, dst, ssem, rsem, **where):
        return pltpu.make_async_remote_copy(
            src_ref=src,
            dst_ref=dst,
            send_sem=ssem,
            recv_sem=rsem,
            device_id=where,
            device_id_type=pl.DeviceIdType.MESH,
        )

    def weight_copy(c, j, half):
        section = (1 - s) if half == 0 else s
        column = (relative(ORDER[j]) * 2 + section) * width + c * sub
        return pltpu.make_async_copy(
            weight_hbm.at[:, pl.ds(pl.multiple_of(column, sub), sub)],
            weight_ring.at[2 * j + half],
            weight_sem.at[2 * j + half],
        )

    def raw_copy(k):
        start = (k % n_block) * width + (k // n_block) * sub
        slot = k % RAW_SLOTS
        return pltpu.make_async_copy(
            gate_up_hbm.at[pl.ds(pl.multiple_of(start, sub), sub)],
            raw_ring.at[slot],
            raw_sem.at[slot],
        )

    def copy0(c, r):
        return remote(
            sent_part.at[c, r], got0.at[c, r], send0.at[c, r], recv0.at[c, r], section=1 - s
        )

    def copy1(c, h):
        return remote(
            kept_part.at[c, 2 * h + 1],
            got1.at[c, h],
            send1.at[c, h],
            recv1.at[c, h],
            tensor=relative(1),
        )

    def copy2(c):
        return remote(
            kept_part.at[c, 2], got2.at[c], send2.at[c], recv2.at[c], tensor=relative(2)
        )

    def copy_block(qq, c, o, sems, **where):
        b = o * 2 + s
        here = blocks.at[qq, c, b]
        return remote(here, here, sems.at[c, o], recv_block.at[qq, c, b], **where)

    def await_block(qq, c, b):
        here = blocks.at[qq, c, b]
        remote(
            here, here, send_own.at[c, 0], recv_block.at[qq, c, b], section=1 - s
        ).wait_recv()

    for j in range(4):
        for half in range(2):
            weight_copy(0, j, half).start()
    barrier = pltpu.get_barrier_semaphore()
    for d in range(1, nt):
        pl.semaphore_signal(barrier, inc=1, device_id={"tensor": (t + d) % nt}, device_id_type=pl.DeviceIdType.MESH)
    pl.semaphore_signal(barrier, inc=1, device_id={"seq": 1 - q}, device_id_type=pl.DeviceIdType.MESH)
    pl.semaphore_signal(barrier, inc=1, device_id={"section": 1 - s}, device_id_type=pl.DeviceIdType.MESH)
    for k in range(RAW_SLOTS):
        raw_copy(k).start()
    pl.semaphore_wait(barrier, nt + 1)

    def project(c):
        for j, r in enumerate(ORDER):
            for half in range(2):
                weight_copy(c, j, half).wait()
                part = jnp.dot(
                    attn_ref[...], weight_ring[2 * j + half], preferred_element_type=f32
                ).astype(bf16)
                (sent_part, kept_part)[half][c, r] = part

                @pl.when(c + 1 < CHUNKS)
                def _():
                    weight_copy(c + 1, j, half).start()

                if half == 0:
                    copy0(c, r).start()

    def add_section(c):
        for r in ORDER:
            copy0(c, r).wait_recv()
            kept_part[c, r] = (
                kept_part[c, r].astype(f32) + got0[c, r].astype(f32)
            ).astype(bf16)
            if r % 2:
                copy1(c, r // 2).start()

    def unpack(c):
        @pl.loop(0, n_block)
        def _(b):
            k = c * n_block + b
            raw_copy(k).wait()
            both = pltpu.einshape("kgn->gkn", raw_ring[k % RAW_SLOTS])
            place = pl.ds(pl.multiple_of(b * sub, sub), sub)
            weights[c, place, :hidden_cols] = both[0]
            weights[c, place, hidden_cols:] = both[1]

            @pl.when(k + RAW_SLOTS < CHUNKS * n_block)
            def _():
                raw_copy(k + RAW_SLOTS).start()

    def add_near(c):
        for h in (1, 0):
            copy1(c, h).wait_recv()
            kept_part[c, 2 * h] = (
                kept_part[c, 2 * h].astype(f32) + got1[c, h].astype(f32)
            ).astype(bf16)
            if h:
                copy2(c).start()

    def finish_stream(c):
        copy2(c).wait_recv()
        projected = (kept_part[c, 0].astype(f32) + got2[c].astype(f32)).astype(bf16)
        columns = pl.ds(pl.multiple_of(c * sub, sub), sub)
        stream = (projected.astype(f32) + residual_ref[:, columns].astype(f32)).astype(bf16)
        blocks[q, c, t * 2 + s] = stream
        stream_ref[:, columns] = stream

        @pl.when(t < nt - 1)
        def _():
            copy_block(q, c, t, send_right, tensor=t + 1).start()

        @pl.when(t > 0)
        def _():
            copy_block(q, c, t, send_left, tensor=t - 1).start()

        copy_block(q, c, t, send_seq, seq=1 - q).start()
        copy_block(q, c, t, send_own, section=1 - s).start()

    def forward(c, d):
        @pl.when(t >= d)
        def _():
            o = t - d
            await_block(q, c, o * 2 + s)

            @pl.when(t < nt - 1)
            def _():
                copy_block(q, c, o, send_right, tensor=t + 1).start()

            copy_block(q, c, o, send_seq, seq=1 - q).start()
            copy_block(q, c, o, send_own, section=1 - s).start()

        @pl.when(t + d < nt)
        def _():
            o = t + d
            await_block(q, c, o * 2 + s)

            @pl.when(t > 0)
            def _():
                copy_block(q, c, o, send_left, tensor=t - 1).start()

            copy_block(q, c, o, send_seq, seq=1 - q).start()
            copy_block(q, c, o, send_own, section=1 - s).start()

    def hand_over(c, d):
        def one(o):
            await_block(1 - q, c, o * 2 + s)
            copy_block(1 - q, c, o, send_other, section=1 - s).start()

        if d == 0:
            one(t)
        else:

            @pl.when(t >= d)
            def _():
                one(t - d)

            @pl.when(t + d < nt)
            def _():
                one(t + d)

    def multiply(qq, c):
        for o in range(nt):
            await_block(qq, c, o * 2 + 1 - s)

        @pl.loop(0, n_block)
        def _(b):
            x = blocks[qq, c, b].astype(f32)
            gain = gain_ref[:, pl.ds(pl.multiple_of(b * width + c * sub, sub), sub)].astype(f32)
            scaled[:, pl.ds(pl.multiple_of(b * sub, sub), sub)] = (x * gain).astype(bf16)
            square = x * x
            total = square[:, :128]
            for k in range(1, sub // 128):
                total = total + square[:, k * 128 : (k + 1) * 128]
            squares[qq] += total

        tile = 512

        @pl.loop(0, 2 * hidden_cols // tile)
        def _(n):
            columns = pl.ds(pl.multiple_of(n * tile, tile), tile)
            acc[qq, :, columns] += jnp.dot(
                scaled[...], weights[c, :, columns], preferred_element_type=f32
            )

    acc[...] = jnp.zeros_like(acc)
    squares[...] = jnp.zeros_like(squares)
    stages = (
        (3, unpack),
        (6, lambda c: multiply(q, c)),
        (7, lambda c: multiply(1 - q, c)),
        (0, project),
        (0, add_section),
        (1, add_near),
        (2, finish_stream),
        (3, lambda c: forward(c, 1)),
        (4, lambda c: forward(c, 2)),
        (5, lambda c: forward(c, 3)),
        (3, lambda c: hand_over(c, 0)),
        (4, lambda c: hand_over(c, 1)),
        (5, lambda c: hand_over(c, 2)),
        (6, lambda c: hand_over(c, 3)),
    )

    @pl.loop(0, CHUNKS + 7)
    def _(step):
        for lag, stage in stages:

            @pl.when(jnp.logical_and(step >= lag, step < lag + CHUNKS))
            def _():
                stage(step - lag)

    for qq in range(2):
        mean_square = jnp.sum(squares[qq], axis=1, keepdims=True) / (n_block * width)
        scale = lax.rsqrt(mean_square + epsilon)
        tile = 256

        @pl.loop(0, hidden_cols // tile)
        def _(n):
            gate = acc[qq, :, pl.ds(pl.multiple_of(n * tile, tile), tile)] * scale
            up = acc[qq, :, pl.ds(pl.multiple_of(hidden_cols + n * tile, tile), tile)] * scale
            hidden_ref[qq * rows : (qq + 1) * rows, pl.ds(pl.multiple_of(n * tile, tile), tile)] = (
                gate / (1.0 + jnp.exp(-gate)) * up
            ).astype(bf16)

    @pl.loop(0, CHUNKS)
    def _(c):
        for r in range(4):
            copy0(c, r).wait_send()
        for h in range(2):
            copy1(c, h).wait_send()
        copy2(c).wait_send()
        for o in range(nt):
            copy_block(q, c, o, send_seq, seq=1 - q).wait_send()
            copy_block(q, c, o, send_own, section=1 - s).wait_send()
            copy_block(1 - q, c, o, send_other, section=1 - s).wait_send()

            @pl.when(jnp.logical_and(o <= t, t < nt - 1))
            def _():
                copy_block(q, c, o, send_right, tensor=(t + 1) % nt).wait_send()

            @pl.when(jnp.logical_and(o >= t, t > 0))
            def _():
                copy_block(q, c, o, send_left, tensor=(t + nt - 1) % nt).wait_send()


def fused(attn_out, residual, out_weight, norm_gain, gate_up):
    rows, width = attn_out.shape
    nt = lax.axis_size("tensor")
    hidden_cols = gate_up.shape[2]
    sub = width // CHUNKS
    depth = gate_up.shape[0] // CHUNKS
    vmem = pl.BlockSpec(memory_space=pltpu.VMEM)
    hbm = pl.BlockSpec(memory_space=pl.ANY)
    dma = pltpu.SemaphoreType.DMA
    bf16, f32 = jnp.bfloat16, jnp.float32
    return pl.pallas_call(
        fused_kernel,
        name="layer_window",
        out_shape=(
            jax.ShapeDtypeStruct((rows, width), bf16),
            jax.ShapeDtypeStruct((2 * rows, hidden_cols), bf16),
        ),
        in_specs=[vmem, vmem, vmem, hbm, hbm],
        out_specs=(vmem, vmem),
        scratch_shapes=[
            pltpu.VMEM((8, width, sub), bf16),
            pltpu.VMEM((RAW_SLOTS, sub, 2, hidden_cols), bf16),
            pltpu.VMEM((CHUNKS, depth, 2 * hidden_cols), bf16),
            pltpu.VMEM((CHUNKS, 4, rows, sub), bf16),
            pltpu.VMEM((CHUNKS, 4, rows, sub), bf16),
            pltpu.VMEM((CHUNKS, 4, rows, sub), bf16),
            pltpu.VMEM((CHUNKS, 2, rows, sub), bf16),
            pltpu.VMEM((CHUNKS, rows, sub), bf16),
            pltpu.VMEM((2, CHUNKS, 2 * nt, rows, sub), bf16),
            pltpu.VMEM((rows, depth), bf16),
            pltpu.VMEM((2, rows, 2 * hidden_cols), f32),
            pltpu.VMEM((2, rows, 128), f32),
            dma((8,)),
            dma((RAW_SLOTS,)),
            dma((CHUNKS, 4)),
            dma((CHUNKS, 4)),
            dma((CHUNKS, 2)),
            dma((CHUNKS, 2)),
            dma((CHUNKS,)),
            dma((CHUNKS,)),
            dma((CHUNKS, nt)),
            dma((CHUNKS, nt)),
            dma((CHUNKS, nt)),
            dma((CHUNKS, nt)),
            dma((CHUNKS, nt)),
            dma((2, CHUNKS, 2 * nt)),
        ],
        compiler_params=pltpu.CompilerParams(
            collective_id=0, has_side_effects=True, vmem_limit_bytes=66 * 1024 * 1024 - 2 * 1024 * 1024 - 65536
        ),
    )(attn_out, residual, norm_gain.reshape(1, -1), out_weight, gate_up)


def fits_fused(mesh, attn_out, gate_up):
    rows, width = attn_out.shape
    return (
        (mesh.shape["tensor"], mesh.shape["seq"], mesh.shape["section"]) == (4, 2, 2)
        and rows % 16 == 0
        and width % (128 * CHUNKS) == 0
        and gate_up.shape[2] % 256 == 0
        and 2 * gate_up.size <= 34 * 1024 * 1024
        and rows * width <= 192 * 1024
    )


def solution(mesh):
    placed = (
        P(("groups", "seq"), ("tensor", "section")),
        P(("groups", "seq"), ("tensor", "section")),
        P(("tensor", "section"), None),
        P(),
        P(None, None, ("tensor", "seq", "section")),
    )
    def step(*args):
        return (fused if fits_fused(mesh, args[0], args[4]) else local)(*args)

    return jax.shard_map(
        step,
        mesh=mesh,
        in_specs=placed,
        out_specs=(
            P(("groups", "seq"), ("tensor", "section")),
            P("groups", ("tensor", "seq", "section")),
        ),
        check_vma=False,
    )
```
